512 devices in a mesh: dp: 8 (over x, y_hi), mp: 64 (over z, y_lo, core).
Axes of the slice: x: 4, y: 4 (y_hi: 2, y_lo: 2; y = y_hi * 2 + y_lo), z: 16, core: 2. Of those that a mesh axis runs over, the one named last changes fastest.
Arguments:
- tokens: bfloat16 [4096, 16384], P('dp', 'mp'), may hold values from -6 to 6
- block_weight: bfloat16 [7, 256, 32768], P(None, None, 'mp'), may hold values from -0.125 to 0.125
- left_factor: bfloat16 [16384, 256], P('mp'), may hold values from -0.046875 to 0.046875
- right_factor: bfloat16 [256, 32768], P(None, 'mp'), may hold values from -0.375 to 0.375
- out_cotangent: bfloat16 [4096, 32768], P('dp', 'mp'), may hold values from -6 to 6
Outputs:
- activated: bfloat16 [4096, 32768], P('dp', 'mp')
- input_grad: bfloat16 [4096, 16384], P('dp', 'mp')
- weight_grad: bfloat16 [7, 256, 32768], P(None, 'dp', 'mp')
- left_grad: bfloat16 [16384, 256], P('mp')
- right_grad: bfloat16 [256, 32768], P(None, 'mp')
The draws below stay inside these ranges and needn't reach their ends.
All inputs are finite; a program needn't handle non-finite values.
Results may differ from the reference program's by a relative error of at most 0.0062.
Values may be sent and summed in bfloat16 or wider, within the bound.
A program may use at most 64 MiB of HBM per device.

```python
import jax
import jax.numpy as jnp
import numpy as np

D = 16384
FF = 32768
B = 256
K = 7
R = 256
TOKENS = 4096


def steps_of(own_key, dims, cuts, low, top_value):
    def one(dim, parts):
        draws = jax.random.uniform(jax.random.fold_in(jax.random.fold_in(own_key, 6), dim), (parts,), jnp.float32, low / len(cuts), top_value / len(cuts))
        return jnp.repeat(jnp.exp(draws), dims[dim] // parts).reshape((-1,) + (1,) * (len(dims) - dim - 1))

    loudness = one(*cuts[0])
    for cut in cuts[1:]:
        loudness = loudness * one(*cut)
    return loudness


def bell_draw(key, dims, scale, reach, shards=(), dtype=jnp.bfloat16):
    array = jax.random.normal(key, dims, jnp.float32) * scale
    if len(shards) > 0:
        array = steps_of(key, dims, shards, -0.22, 0.18) * array
    return jnp.clip(array, min=-reach, max=reach).astype(dtype)


def setup_inputs(seed: int = 0) -> dict:
    seeds = jax.random.split(jax.random.key(seed), 6)
    tokens = bell_draw(seeds[0], (TOKENS, D), 1.0, 6.0, ((0, 8), (1, 64)))
    block_weight = bell_draw(seeds[1], (K, B, FF), (K * B) ** -0.5, 0.125, ((2, 64),))
    left_factor = bell_draw(seeds[2], (D, R), D ** -0.5, 0.046875, ((0, 64),))
    right_factor = bell_draw(seeds[3], (R, FF), R ** -0.5, 0.375, ((1, 64),))
    out_cotangent = bell_draw(seeds[4], (TOKENS, FF), 1.0, 6.0, ((0, 8), (1, 64)))
    return dict(tokens=tokens, block_weight=block_weight, left_factor=left_factor, right_factor=right_factor, out_cotangent=out_cotangent)


gelu_scale = 0.7978845608028654
gelu_cubic = 0.044715


def gelu_parts(preact):
    inner = gelu_scale * (preact + gelu_cubic * preact * preact * preact)
    tangent = jnp.tanh(inner)
    value = 0.5 * preact * (1.0 + tangent)
    slope = 0.5 * (1.0 + tangent) + 0.5 * preact * (1.0 - tangent * tangent) * gelu_scale * (1.0 + 3.0 * gelu_cubic * preact * preact)
    return value, slope


def reference(tokens, block_weight, left_factor, right_factor, out_cotangent):
    tok_count = tokens.shape[0]
    group_count = D // B
    group_ids = np.arange(group_count)
    tok_blocks = tokens.reshape(tok_count, group_count, B)
    weight_views = block_weight.reshape(K, B, group_count, 2 * B)
    butterfly = jnp.zeros((tok_count, group_count, 2 * B), jnp.float32)
    for tap_index in range(K):
        offset = 0 if tap_index == 0 else 1 << (tap_index - 1)
        chosen = tok_blocks[:, group_ids ^ offset].astype(jnp.float32)
        butterfly = butterfly + jnp.einsum("ngc,cgh->ngh", chosen, weight_views[tap_index].astype(jnp.float32))
    latent = jnp.dot(tokens, left_factor, preferred_element_type=jnp.float32)
    latent_bf = latent.astype(jnp.bfloat16)
    preact = butterfly.reshape(tok_count, FF) + jnp.dot(latent_bf, right_factor, preferred_element_type=jnp.float32)
    value, slope = gelu_parts(preact)
    activated = value.astype(jnp.bfloat16)
    grad_pre = (out_cotangent.astype(jnp.float32) * slope).astype(jnp.bfloat16)
    latent_grad = jnp.dot(grad_pre, right_factor.T, preferred_element_type=jnp.float32).astype(jnp.bfloat16)
    left_grad = jnp.dot(tokens.T, latent_grad, preferred_element_type=jnp.float32).astype(jnp.bfloat16)
    right_grad = jnp.dot(latent_bf.T, grad_pre, preferred_element_type=jnp.float32).astype(jnp.bfloat16)
    grad_view = grad_pre.reshape(tok_count, group_count, 2 * B).astype(jnp.float32)
    input_grad = jnp.dot(latent_grad, left_factor.T, preferred_element_type=jnp.float32).reshape(tok_count, group_count, B)
    weight_parts = []
    for tap_index in range(K):
        offset = 0 if tap_index == 0 else 1 << (tap_index - 1)
        chosen = tok_blocks[:, group_ids ^ offset].astype(jnp.float32)
        weight_tap = weight_views[tap_index].astype(jnp.float32)
        contrib = jnp.einsum("ngh,cgh->ngc", grad_view, weight_tap)
        input_grad = input_grad + contrib[:, group_ids ^ offset]
        weight_parts.append(jnp.einsum("ngc,ngh->cgh", chosen, grad_view).reshape(B, FF))
    weight_grad = jnp.stack(weight_parts).astype(jnp.bfloat16)
    input_grad = input_grad.reshape(tok_count, D).astype(jnp.bfloat16)
    return activated, input_grad, weight_grad, left_grad, right_grad
```

```python
import functools

import jax
import jax.numpy as jnp
from jax import lax
from jax.experimental import pallas as pl
from jax.experimental.pallas import tpu as pltpu
from jax.sharding import PartitionSpec as P

gelu_scale = 0.7978845608028654
gelu_cubic = 0.044715
F32 = jnp.float32
BF16 = jnp.bfloat16

AR_CORE, AR_Y, AG_Y, AG_CORE, LEG_UP, LEG_DOWN, FAR_UP, FAR_DOWN, HALF_A, HALF_B, TAP = range(11)


def gelu_parts(preact):
    inner = gelu_scale * (preact + gelu_cubic * preact * preact * preact)
    tangent = jnp.tanh(inner)
    value = 0.5 * preact * (1.0 + tangent)
    slope = 0.5 * (1.0 + tangent) + 0.5 * preact * (1.0 - tangent * tangent) * gelu_scale * (
        1.0 + 3.0 * gelu_cubic * preact * preact
    )
    return value, slope


def mm(a, b):
    return lax.dot_general(a, b, (((1,), (0,)), ((), ())), preferred_element_type=F32)


def mm_nt(a, b):
    return lax.dot_general(a, b, (((1,), (1,)), ((), ())), preferred_element_type=F32)


def mm_tn(a, b):
    return lax.dot_general(a, b, (((0,), (0,)), ((), ())), preferred_element_type=F32)


def kernel(
    Z, ND,
    tok_h, w_h, left_h, right_h, cot_h,
    act_h, ig_h, wg_h, lg_h, rg_h,
    tok_v, w_v, left_v, right_v, cot_v,
    acc, act_v, gp_v,
    part, rx_core, half, rx_y, z_send, z_recv, gathered, lat,
    taps, spread, relay, iacc, ig_v,
    wg_send, wg_recv, wg_out, rg_all, left_send, left_recv, left_out, lg_all,
    one_send, one_recv, zs_send, zs_recv, d_send, d_recv, local,
):
    T, C = tok_v.shape
    R, H = right_v.shape
    K = w_v.shape[0]
    T2, T4 = T // 2, T // 4
    RB = C // ND
    NC = R // 128
    top, second = K - 1, K - 2

    d = lax.axis_index("dp")
    m = lax.axis_index("mp")
    c = lax.rem(m, 2)
    y = lax.rem(lax.div(m, 2), 2)
    z = lax.div(m, 4)
    base = m - z * 4

    def flip(stride):
        return m + stride - 2 * stride * lax.rem(lax.div(m, stride), 2)

    def z_at(k):
        return base + 4 * lax.rem(z + k, Z)

    core_peer, y_peer = flip(1), flip(2)

    def to(src, dst, send, recv, **where):
        return pltpu.make_async_remote_copy(
            src_ref=src, dst_ref=dst, send_sem=send, recv_sem=recv,
            device_id=where, device_id_type=pl.DeviceIdType.MESH,
        )

    def one(ph, k, src, dst, peer):
        return to(src, dst, one_send.at[ph, k], one_recv.at[ph, k], mp=peer)

    barrier = pltpu.get_barrier_semaphore()

    def greet(**where):
        pl.semaphore_signal(barrier, inc=1, device_id=where, device_id_type=pl.DeviceIdType.MESH)

    @pl.loop(1, Z)
    def _(k):
        greet(mp=z_at(k))

    @pl.loop(1, ND)
    def _(k):
        greet(dp=lax.rem(d + k, ND))

    greet(mp=core_peer)
    greet(mp=y_peer)

    loads = [
        pltpu.make_async_copy(src, dst, local.at[i])
        for i, (src, dst) in enumerate(
            [(tok_h, tok_v), (left_h, left_v), (w_h, w_v), (right_h, right_v), (cot_h, cot_v)]
        )
    ]
    for load in loads:
        load.start()

    def ar_core(ph):
        return one(ph, AR_CORE, part.at[ph, 1 - c], rx_core.at[ph], core_peer)

    def ar_y(ph):
        return one(ph, AR_Y, half.at[ph, 1 - y], rx_y.at[ph], y_peer)

    def ag_y(ph):
        return one(ph, AG_Y, gathered.at[ph, c, y], gathered.at[ph, c, y], y_peer)

    def ag_core(ph):
        return one(ph, AG_CORE, gathered.at[ph, c], gathered.at[ph, c], core_peer)

    def z_scatter(ph, k):
        there = lax.rem(z + k, Z)
        return to(
            z_send.at[ph, there], z_recv.at[ph, z], zs_send.at[ph, 0, there], zs_recv.at[ph, 0, z],
            mp=z_at(k),
        )

    def z_scatter_in(ph, k):
        there = lax.rem(z + k, Z)
        return to(
            z_send.at[ph, there], z_recv.at[ph, there], zs_send.at[ph, 0, there],
            zs_recv.at[ph, 0, there], mp=z_at(k),
        )

    def z_gather(ph, k):
        there = lax.rem(z + k, Z)
        return to(
            gathered.at[ph, c, y, z], gathered.at[ph, c, y, z], zs_send.at[ph, 1, there],
            zs_recv.at[ph, 1, z], mp=z_at(k),
        )

    def z_gather_in(ph, k):
        there = lax.rem(z + k, Z)
        return to(
            gathered.at[ph, c, y, there], gathered.at[ph, c, y, there], zs_send.at[ph, 1, there],
            zs_recv.at[ph, 1, there], mp=z_at(k),
        )

    def tap_src(ph, t):
        return tok_h if ph == 0 else spread.at[t - 1]

    def leg(ph, up):
        rows = pl.ds(0 if up else T2, T2)
        return one(
            ph, LEG_UP if up else LEG_DOWN, tap_src(ph, top).at[rows], relay.at[ph, 0 if up else 1],
            z_at(Z // 4 if up else Z - Z // 4),
        )

    def far(ph, up):
        rows = pl.ds(0 if up else T2, T2)
        return one(
            ph, FAR_UP if up else FAR_DOWN, relay.at[ph, 0 if up else 1],
            taps.at[ph, top - 1, rows], z_at(Z // 4 if up else Z - Z // 4),
        )

    def half_tap(ph, which):
        rows = pl.ds(which * T2, T2)
        return one(
            ph, HALF_A + which, tap_src(ph, second).at[rows], taps.at[ph, second - 1, rows],
            flip(1 << (second - 1)),
        )

    def tap(ph, t):
        return one(ph, TAP + t - 1, tap_src(ph, t), taps.at[ph, t - 1], flip(1 << (t - 1)))

    near = list(range(second - 1, 2, -1))

    def after_core(ph):
        ar_core(ph).wait_recv()
        for i in range(2):
            rows = pl.ds(i * T4, T4)
            half[ph, i] = part[ph, c, rows] + rx_core[ph, rows]
        ar_y(ph).start()

    def after_y(ph):
        ar_y(ph).wait_recv()
        for rb in range(T4 // 16):
            rows = pl.ds(rb * 16, 16)
            total = (half[ph, y, rows] + rx_y[ph, rows]).astype(BF16)
            for ch in range(NC):
                z_send[ph, rb * NC + ch] = total[:, ch * 128 : (ch + 1) * 128]
        z_recv[ph, z] = z_send[ph, z]

        @pl.loop(1, Z)
        def _(k):
            z_scatter(ph, k).start()

    def after_scatter(ph):
        @pl.loop(1, Z)
        def _(k):
            z_scatter_in(ph, k).wait_recv()

        total = z_recv[ph, 0].astype(F32)
        for i in range(1, Z):
            total = total + z_recv[ph, i].astype(F32)
        gathered[ph, c, y, z] = total.astype(BF16)

        @pl.loop(1, Z)
        def _(k):
            z_gather(ph, k).start()

    def after_gather(ph):
        @pl.loop(1, Z)
        def _(k):
            z_gather_in(ph, k).wait_recv()

        ag_y(ph).start()
        one(ph, AG_Y, gathered.at[ph, c, 1 - y], gathered.at[ph, c, 1 - y], y_peer).wait_recv()
        ag_core(ph).start()
        one(ph, AG_CORE, gathered.at[ph, 1 - c], gathered.at[ph, 1 - c], core_peer).wait_recv()
        for i in range(2):
            for j in range(2):
                for rb in range(T4 // 16):
                    for ch in range(NC):
                        lat[ph, pl.ds(i * T2 + j * T4 + rb * 16, 16), pl.ds(ch * 128, 128)] = (
                            gathered[ph, i, j, rb * NC + ch]
                        )

    def forward_far(ph):
        for up in (True, False):
            leg(ph, up).wait_recv()
            far(ph, up).start()

    def wait_tap(ph, t):
        if t == top:
            far(ph, True).wait_recv()
            far(ph, False).wait_recv()
        elif t == second:
            half_tap(ph, 0).wait_recv()
            half_tap(ph, 1).wait_recv()
        else:
            tap(ph, t).wait_recv()

    loads[0].wait()
    loads[1].wait()
    partial = mm(tok_v[...], left_v[...])
    part[0, 0] = partial[:T2]
    part[0, 1] = partial[T2:]
    pl.semaphore_wait(barrier, Z - 1 + ND - 1 + 2)
    ar_core(0).start()
    leg(0, True).start()
    leg(0, False).start()
    after_core(0)
    tap(0, 1).start()
    tap(0, 2).start()
    loads[2].wait()
    acc[...] = mm(tok_v[...], w_v[0])
    after_y(0)
    half_tap(0, 0).start()
    forward_far(0)
    for t in (1, 2):
        wait_tap(0, t)
        acc[...] += mm(taps[0, t - 1], w_v[t])
    after_scatter(0)
    half_tap(0, 1).start()
    for t in near:
        tap(0, t).start()
    after_gather(0)
    loads[3].wait()
    acc[...] += mm(lat[0], right_v[...])
    for t in near[::-1] + [second, top]:
        wait_tap(0, t)
        acc[...] += mm(taps[0, t - 1], w_v[t])
    loads[4].wait()

    @pl.loop(0, T // 32)
    def _(i):
        rows = pl.ds(pl.multiple_of(i * 32, 32), 32)
        value, slope = gelu_parts(acc[rows])
        act_v[rows] = value.astype(BF16)
        gp_v[rows] = (cot_v[rows].astype(F32) * slope).astype(BF16)

    stores = [pltpu.make_async_copy(act_v, act_h, local.at[5])]
    stores[0].start()

    def fill(t):
        spread[t - 1] = mm_nt(gp_v[...], w_v[t]).astype(BF16)

    fill(top)
    partial = mm_nt(gp_v[...], right_v[...])
    part[1, 0] = partial[:T2]
    part[1, 1] = partial[T2:]
    leg(1, True).start()
    leg(1, False).start()
    fill(second)
    ar_core(1).start()
    fill(1)
    after_core(1)
    fill(2)
    tap(1, 1).start()
    after_y(1)
    half_tap(1, 0).start()
    tap(1, 2).start()

    for t in range(K):
        source = tok_v[...] if t == 0 else taps[0, t - 1]
        wg_send[:, t] = mm_tn(source, gp_v[...]).astype(BF16).reshape(ND, RB, H)
    wg_send[:, K] = mm_tn(lat[0], gp_v[...]).astype(BF16).reshape(ND, RB, H)

    def dp_copy(row, k, src, dst, incoming):
        there = lax.rem(d + k, ND)
        return to(
            src(there), dst(there if incoming else d), d_send.at[row, there],
            d_recv.at[row, there if incoming else d], dp=there,
        )

    def wg_copy(k, incoming=False):
        return dp_copy(0, k, lambda p: wg_send.at[p], lambda p: wg_recv.at[p], incoming)

    def rg_copy(k, incoming=False):
        return dp_copy(1, k, lambda p: wg_out.at[K], lambda p: rg_all.at[p], incoming)

    def ls_copy(k, incoming=False):
        return dp_copy(2, k, lambda p: left_send.at[p], lambda p: left_recv.at[p], incoming)

    def lg_copy(k, incoming=False):
        return dp_copy(3, k, lambda p: left_out, lambda p: lg_all.at[p], incoming)

    def start_all(make):
        @pl.loop(1, ND)
        def _(k):
            make(k).start()

    def receive_all(make):
        @pl.loop(1, ND)
        def _(k):
            make(k, True).wait_recv()

    wg_recv[d] = wg_send[d]
    start_all(wg_copy)
    for t in near:
        fill(t)
    forward_far(1)
    after_scatter(1)
    half_tap(1, 1).start()
    for t in near:
        tap(1, t).start()
    iacc[...] = mm_nt(gp_v[...], w_v[0])
    for t in (1, 2):
        wait_tap(1, t)
        iacc[...] += taps[1, t - 1].astype(F32)
    after_gather(1)
    left_send[...] = mm_tn(tok_v[...], lat[1]).astype(BF16).reshape(ND, RB, R)
    left_recv[d] = left_send[d]
    start_all(ls_copy)
    iacc[...] += mm_nt(lat[1], left_v[...])
    receive_all(wg_copy)

    @pl.loop(0, K + 1)
    def _(t):
        total = wg_recv[0, t].astype(F32)
        for i in range(1, ND):
            total = total + wg_recv[i, t].astype(F32)
        wg_out[t] = total.astype(BF16)

    rg_all[d] = wg_out[K]
    start_all(rg_copy)
    stores.append(pltpu.make_async_copy(wg_out.at[pl.ds(0, K)], wg_h, local.at[6]))
    stores[-1].start()
    receive_all(ls_copy)
    total = left_recv[0].astype(F32)
    for i in range(1, ND):
        total = total + left_recv[i].astype(F32)
    left_out[...] = total.astype(BF16)
    lg_all[d] = left_out[...]
    start_all(lg_copy)
    for t in near[::-1] + [second]:
        wait_tap(1, t)
        iacc[...] += taps[1, t - 1].astype(F32)
    receive_all(rg_copy)
    stores.append(pltpu.make_async_copy(rg_all, rg_h, local.at[7]))
    stores[-1].start()
    receive_all(lg_copy)
    stores.append(pltpu.make_async_copy(lg_all, lg_h, local.at[8]))
    stores[-1].start()
    wait_tap(1, top)
    ig_v[...] = (iacc[...] + taps[1, top - 1].astype(F32)).astype(BF16)
    stores.append(pltpu.make_async_copy(ig_v, ig_h, local.at[9]))
    stores[-1].start()

    for ph in range(2):
        for copy in (ar_core, ar_y, ag_y, ag_core):
            copy(ph).wait_send()
        for up in (True, False):
            leg(ph, up).wait_send()
            far(ph, up).wait_send()
        for which in range(2):
            half_tap(ph, which).wait_send()
        for t in [1, 2] + near:
            tap(ph, t).wait_send()

        @pl.loop(1, Z)
        def _(k):
            z_scatter(ph, k).wait_send()
            z_gather(ph, k).wait_send()

    @pl.loop(1, ND)
    def _(k):
        for copy in (wg_copy, rg_copy, ls_copy, lg_copy):
            copy(k).wait_send()

    for store in stores:
        store.wait()


def on_device(tokens, block_weight, left_factor, right_factor, out_cotangent):
    ND = lax.axis_size("dp")
    Z = lax.axis_size("mp") // 4
    T, C = tokens.shape
    K, _, H = block_weight.shape
    R = right_factor.shape[0]
    RB = C // ND
    any_spec = pl.BlockSpec(memory_space=pl.ANY)
    bf = lambda *shape: pltpu.VMEM(shape, BF16)
    fl = lambda *shape: pltpu.VMEM(shape, F32)
    dma = lambda *shape: pltpu.SemaphoreType.DMA(shape)
    out = lambda *shape: jax.ShapeDtypeStruct(shape, BF16)
    act, ig, wg, lg, rg = pl.pallas_call(
        functools.partial(kernel, Z, ND),
        out_shape=(out(T, H), out(T, C), out(K, RB, H), out(ND, RB, R), out(ND, RB, H)),
        in_specs=[any_spec] * 5,
        out_specs=[any_spec] * 5,
        scratch_shapes=[
            bf(T, C), bf(K, C, H), bf(C, R), bf(R, H), bf(T, H),
            fl(T, H), bf(T, H), bf(T, H),
            fl(2, 2, T // 2, R), fl(2, T // 2, R), fl(2, 2, T // 4, R), fl(2, T // 4, R),
            bf(2, Z, 16, 128), bf(2, Z, 16, 128), bf(2, 2, 2, Z, 16, 128), bf(2, T, R),
            bf(2, K - 1, T, C), bf(K - 1, T, C), bf(2, 2, T // 2, C), fl(T, C), bf(T, C),
            bf(ND, K + 1, RB, H), bf(ND, K + 1, RB, H), bf(K + 1, RB, H), bf(ND, RB, H),
            bf(ND, RB, R), bf(ND, RB, R), bf(RB, R), bf(ND, RB, R),
            dma(2, TAP + K - 1), dma(2, TAP + K - 1), dma(2, 2, Z), dma(2, 2, Z),
            dma(4, ND), dma(4, ND), dma(10),
        ],
        compiler_params=pltpu.CompilerParams(
            collective_id=0, has_side_effects=True, vmem_limit_bytes=56 * 1024 * 1024
        ),
    )(tokens, block_weight, left_factor, right_factor, out_cotangent)
    return act, ig, wg, lg.reshape(C, R), rg.reshape(R, H)


def solution(mesh):
    return jax.shard_map(
        on_device,
        mesh=mesh,
        in_specs=(P("dp", "mp"), P(None, None, "mp"), P("mp", None), P(None, "mp"), P("dp", "mp")),
        out_specs=(P("dp", "mp"), P("dp", "mp"), P(None, "dp", "mp"), P("mp", None), P(None, "mp")),
        check_vma=False,
    )
```

```python
import functools

import jax
import jax.numpy as jnp
from jax import lax
from jax.experimental import pallas as pl
from jax.experimental.pallas import tpu as pltpu
from jax.sharding import PartitionSpec as P

gelu_scale = 0.7978845608028654
gelu_cubic = 0.044715
F32 = jnp.float32
BF16 = jnp.bfloat16

AR_CORE, AR_Y, AG_Y, AG_CORE, TAP_CORE, TAP_Y = range(6)
NQ = 4


def gelu_parts(preact):
    inner = gelu_scale * (preact + gelu_cubic * preact * preact * preact)
    tangent = jnp.tanh(inner)
    value = 0.5 * preact * (1.0 + tangent)
    slope = 0.5 * (1.0 + tangent) + 0.5 * preact * (1.0 - tangent * tangent) * gelu_scale * (
        1.0 + 3.0 * gelu_cubic * preact * preact
    )
    return value, slope


def mm(a, b):
    return lax.dot_general(a, b, (((1,), (0,)), ((), ())), preferred_element_type=F32)


def mm_nt(a, b):
    return lax.dot_general(a, b, (((1,), (1,)), ((), ())), preferred_element_type=F32)


def mm_tn(a, b):
    return lax.dot_general(a, b, (((0,), (0,)), ((), ())), preferred_element_type=F32)


def kernel(
    Z, ND,
    tok_h, w_h, left_h, right_h, cot_h,
    act_h, ig_h, wg_h, lg_h, rg_h,
    tok_v, w_v, left_v, right_v, cot_v,
    acc, act_v, gp_v,
    part, rx_core, half, half_send, rx_y, z_send, z_recv, gathered, lat,
    taps, near_out, near_in, own, chain_out, chain_in, iacc, ig_v,
    wg_send, wg_recv, wg_out, rg_all, left_send, left_recv, left_out, lg_all,
    one_send, one_recv, zs_send, zs_recv, f_send, f_recv, b_send, b_recv, d_send, d_recv, local,
):
    T, C = tok_v.shape
    R, H = right_v.shape
    K = w_v.shape[0]
    T2, T4, TQ = T // 2, T // 4, T // NQ
    RB = C // ND
    NC = R // 128
    nz = K - 3
    top = nz - 1

    d = lax.axis_index("dp")
    m = lax.axis_index("mp")
    c = lax.rem(m, 2)
    y = lax.rem(lax.div(m, 2), 2)
    z = lax.div(m, 4)
    base = m - z * 4

    def flip(stride):
        return m + stride - 2 * stride * lax.rem(lax.div(m, stride), 2)

    def z_at(k):
        return base + 4 * lax.rem(z + k, Z)

    core_peer, y_peer = flip(1), flip(2)

    def to(src, dst, send, recv, **where):
        return pltpu.make_async_remote_copy(
            src_ref=src, dst_ref=dst, send_sem=send, recv_sem=recv,
            device_id=where, device_id_type=pl.DeviceIdType.MESH,
        )

    def one(ph, k, src, dst, peer):
        return to(src, dst, one_send.at[ph, k], one_recv.at[ph, k], mp=peer)

    barrier = pltpu.get_barrier_semaphore()

    def greet(**where):
        pl.semaphore_signal(barrier, inc=1, device_id=where, device_id_type=pl.DeviceIdType.MESH)

    @pl.loop(1, Z)
    def _(k):
        greet(mp=z_at(k))

    @pl.loop(1, ND)
    def _(k):
        greet(dp=lax.rem(d + k, ND))

    greet(mp=core_peer)
    greet(mp=y_peer)

    loads = [
        pltpu.make_async_copy(src, dst, local.at[i])
        for i, (src, dst) in enumerate(
            [(tok_h, tok_v), (left_h, left_v), (w_h, w_v), (right_h, right_v), (cot_h, cot_v)]
        )
    ]
    for load in loads:
        load.start()

    def ar_core(ph):
        return one(ph, AR_CORE, part.at[ph, 1 - c], rx_core.at[ph], core_peer)

    def ar_y(ph):
        return one(ph, AR_Y, half_send.at[ph, 1 - y], rx_y.at[ph], y_peer)

    def ag_y(ph):
        return one(ph, AG_Y, gathered.at[ph, c, y], gathered.at[ph, c, y], y_peer)

    def ag_core(ph):
        return one(ph, AG_CORE, gathered.at[ph, c], gathered.at[ph, c], core_peer)

    def z_scatter(ph, k):
        there = lax.rem(z + k, Z)
        return to(
            z_send.at[ph, there], z_recv.at[ph, z], zs_send.at[ph, 0, there], zs_recv.at[ph, 0, z],
            mp=z_at(k),
        )

    def z_scatter_in(ph, k):
        there = lax.rem(z + k, Z)
        return to(
            z_send.at[ph, there], z_recv.at[ph, there], zs_send.at[ph, 0, there],
            zs_recv.at[ph, 0, there], mp=z_at(k),
        )

    def z_gather(ph, k):
        there = lax.rem(z + k, Z)
        return to(
            gathered.at[ph, c, y, z], gathered.at[ph, c, y, z], zs_send.at[ph, 1, there],
            zs_recv.at[ph, 1, z], mp=z_at(k),
        )

    def z_gather_in(ph, k):
        there = lax.rem(z + k, Z)
        return to(
            gathered.at[ph, c, y, there], gathered.at[ph, c, y, there], zs_send.at[ph, 1, there],
            zs_recv.at[ph, 1, there], mp=z_at(k),
        )

    def near_tap(ph, k):
        src = tok_h if ph == 0 else near_out.at[k]
        dst = taps.at[k] if ph == 0 else near_in.at[k]
        return one(ph, TAP_CORE + k, src, dst, flip(1 << k))

    def rows_of(q):
        return pl.ds(q * TQ, TQ)

    def z_flip(at, k):
        return at + (1 << k) - (2 << k) * lax.rem(lax.div(at, 1 << k), 2)

    def way(at, k):
        return lax.rem(lax.div(at, 1 << k), 2)

    onward = z_flip(z_flip(z, top - 1), top)

    def z_tap(s, q):
        return to(
            tok_h.at[rows_of(q)], taps.at[2 + s, rows_of(q)], f_send.at[s, q], f_recv.at[s, q],
            mp=base + 4 * z_flip(z, s),
        )

    def z_pass(q):
        return to(
            taps.at[1 + top, rows_of(q)], taps.at[2 + top, rows_of(q)], f_send.at[top, q],
            f_recv.at[top, q], mp=base + 4 * onward,
        )

    def pass_on(q):
        z_tap(top - 1, q).wait_recv()
        z_pass(q).start()

    def arrived(s, q):
        (z_pass(q) if s == top else z_tap(s, q)).wait_recv()

    def term(s, q):
        peer = onward if s == top else z_flip(z, s)
        return to(
            chain_out.at[s, rows_of(q)], chain_in.at[s, rows_of(q)], b_send.at[s, q],
            b_recv.at[s, q], mp=base + 4 * peer,
        )

    def add_on(q):
        term(top, q).wait_recv()
        rows = rows_of(q)
        chain_out[top - 1, rows] = (own[rows] + chain_in[top, rows].astype(F32)).astype(BF16)
        term(top - 1, q).start()

    def after_core(ph):
        ar_core(ph).wait_recv()
        for i in range(2):
            rows = pl.ds(i * T4, T4)
            both = part[ph, c, rows] + rx_core[ph, rows]
            half[ph, i] = both
            half_send[ph, i] = both.astype(BF16)
        ar_y(ph).start()

    def after_y(ph):
        ar_y(ph).wait_recv()
        for rb in range(T4 // 16):
            rows = pl.ds(rb * 16, 16)
            total = (half[ph, y, rows] + rx_y[ph, rows].astype(F32)).astype(BF16)
            for ch in range(NC):
                z_send[ph, rb * NC + ch] = total[:, ch * 128 : (ch + 1) * 128]
        z_recv[ph, z] = z_send[ph, z]

        @pl.loop(1, Z)
        def _(k):
            z_scatter(ph, k).start()

    def after_scatter(ph):
        @pl.loop(1, Z)
        def _(k):
            z_scatter_in(ph, k).wait_recv()

        total = z_recv[ph, 0].astype(F32)
        for i in range(1, Z):
            total = total + z_recv[ph, i].astype(F32)
        gathered[ph, c, y, z] = total.astype(BF16)

        @pl.loop(1, Z)
        def _(k):
            z_gather(ph, k).start()

    def after_gather(ph):
        @pl.loop(1, Z)
        def _(k):
            z_gather_in(ph, k).wait_recv()

        ag_y(ph).start()

    def after_gather_y(ph):
        one(ph, AG_Y, gathered.at[ph, c, 1 - y], gathered.at[ph, c, 1 - y], y_peer).wait_recv()
        ag_core(ph).start()

    def after_gather_core(ph):
        one(ph, AG_CORE, gathered.at[ph, 1 - c], gathered.at[ph, 1 - c], core_peer).wait_recv()
        for i in range(2):
            for j in range(2):
                for rb in range(T4 // 16):
                    for ch in range(NC):
                        lat[ph, pl.ds(i * T2 + j * T4 + rb * 16, 16), pl.ds(ch * 128, 128)] = (
                            gathered[ph, i, j, rb * NC + ch]
                        )

    loads[0].wait()
    loads[1].wait()
    partial = mm(tok_v[...], left_v[...])
    part[0, 0] = partial[:T2]
    part[0, 1] = partial[T2:]
    pl.semaphore_wait(barrier, Z - 1 + ND - 1 + 2)
    inner = way(z, top - 2) + way(z, top - 1) - 2 * way(z, top - 2) * way(z, top - 1)

    def when_early(ph, queue, quarters):
        @pl.when(inner == 1 - ph)
        def _():
            for q in quarters:
                queue(q)

    def when_late(ph, queue, quarters):
        when_early(1 - ph, queue, quarters)

    ar_core(0).start()
    z_tap(top - 1, 0).start()
    after_core(0)
    near_tap(0, 0).start()
    loads[2].wait()
    acc[...] = mm(tok_v[...], w_v[0])
    after_y(0)
    z_tap(top - 1, 1).start()
    near_tap(0, 1).start()
    pass_on(0)
    after_scatter(0)
    for q in range(2, NQ):
        z_tap(top - 1, q).start()
    for s in range(top - 1):
        for q in range(NQ):
            z_tap(s, q).start()
    pass_on(1)
    for k in range(2):
        near_tap(0, k).wait_recv()
        acc[...] += mm(taps[k], w_v[1 + k])
    when_early(0, pass_on, (2, 3))
    after_gather(0)
    when_late(0, pass_on, (2,))
    loads[3].wait()
    loads[4].wait()
    after_gather_y(0)
    when_late(0, pass_on, (3,))
    acc[...] += mm(taps[1 + top], w_v[2 + top])
    after_gather_core(0)
    acc[...] += mm(lat[0], right_v[...])
    for s in range(top - 1):
        for q in range(NQ):
            arrived(s, q)
        acc[...] += mm(taps[2 + s], w_v[3 + s])

    stores = []
    for q in range(NQ):
        rows = rows_of(q)
        arrived(top, q)
        acc[rows] += mm(taps[2 + top, rows], w_v[3 + top])

        @pl.loop(0, TQ // 32)
        def _(i):
            here = pl.ds(pl.multiple_of(q * TQ + i * 32, 32), 32)
            value, slope = gelu_parts(acc[here])
            act_v[here] = value.astype(BF16)
            gp_v[here] = (cot_v[here].astype(F32) * slope).astype(BF16)

        chain_out[top, rows] = mm_nt(gp_v[rows], w_v[3 + top]).astype(BF16)
        if q == 0:
            term(top, q).start()

    stores = [pltpu.make_async_copy(act_v, act_h, local.at[5])]
    stores[0].start()
    partial = mm_nt(gp_v[...], right_v[...])
    part[1, 0] = partial[:T2]
    part[1, 1] = partial[T2:]
    ar_core(1).start()

    def fill(s):
        chain_out[s] = mm_nt(gp_v[...], w_v[3 + s]).astype(BF16)

    def fill_near(k):
        near_out[k] = mm_nt(gp_v[...], w_v[1 + k]).astype(BF16)

    def fill_weight(t):
        if t == K:
            source = lat[0]
        elif t == 0:
            source = tok_v[...]
        else:
            source = taps[t - 1]
        wg_send[:, t] = mm_tn(source, gp_v[...]).astype(BF16).reshape(ND, RB, H)

    def dp_copy(row, k, src, dst, incoming):
        there = lax.rem(d + k, ND)
        return to(
            src(there), dst(there if incoming else d), d_send.at[row, there],
            d_recv.at[row, there if incoming else d], dp=there,
        )

    KH = (K + 1) // 2

    def wg_copy(part_no, k, incoming=False):
        planes = pl.ds(0, KH) if part_no == 0 else pl.ds(KH, K + 1 - KH)
        return dp_copy(
            4 * part_no, k, lambda p: wg_send.at[p, planes], lambda p: wg_recv.at[p, planes], incoming
        )

    wg_first = functools.partial(wg_copy, 0)
    wg_second = functools.partial(wg_copy, 1)

    def rg_copy(k, incoming=False):
        return dp_copy(1, k, lambda p: wg_out.at[K], lambda p: rg_all.at[p], incoming)

    def ls_copy(k, incoming=False):
        return dp_copy(2, k, lambda p: left_send.at[p], lambda p: left_recv.at[p], incoming)

    def lg_copy(k, incoming=False):
        return dp_copy(3, k, lambda p: left_out, lambda p: lg_all.at[p], incoming)

    def start_all(make):
        @pl.loop(1, ND)
        def _(k):
            make(k).start()

    def receive_all(make):
        @pl.loop(1, ND)
        def _(k):
            make(k, True).wait_recv()

    own[...] = mm_nt(gp_v[...], w_v[2 + top])
    after_core(1)
    fill_near(0)
    near_tap(1, 0).start()
    fill_near(1)
    for s in range(top - 1):
        fill(s)
    for t in range(2):
        fill_weight(t)
    after_y(1)
    term(top, 1).start()
    near_tap(1, 1).start()
    for t in range(2, KH):
        fill_weight(t)
    start_all(wg_first)
    add_on(0)
    for t in range(KH, K + 1):
        fill_weight(t)
    start_all(wg_second)
    wg_recv[d] = wg_send[d]
    iacc[...] = mm_nt(gp_v[...], w_v[0])
    after_scatter(1)
    for q in range(2, NQ):
        term(top, q).start()
    for s in range(top - 1):
        for q in range(NQ):
            term(s, q).start()
    add_on(1)
    when_early(1, add_on, (2, 3))
    after_gather(1)
    when_late(1, add_on, (2,))
    after_gather_y(1)
    when_late(1, add_on, (3,))
    after_gather_core(1)
    left_send[...] = mm_tn(tok_v[...], lat[1]).astype(BF16).reshape(ND, RB, R)
    left_recv[d] = left_send[d]
    start_all(ls_copy)
    iacc[...] += mm_nt(lat[1], left_v[...])
    for k in range(2):
        near_tap(1, k).wait_recv()
        iacc[...] += near_in[k].astype(F32)
    receive_all(wg_first)
    receive_all(wg_second)

    @pl.loop(0, K + 1)
    def _(t):
        total = wg_recv[0, t].astype(F32)
        for i in range(1, ND):
            total = total + wg_recv[i, t].astype(F32)
        wg_out[t] = total.astype(BF16)

    rg_all[d] = wg_out[K]
    start_all(rg_copy)
    stores.append(pltpu.make_async_copy(wg_out.at[pl.ds(0, K)], wg_h, local.at[6]))
    stores[-1].start()
    receive_all(ls_copy)
    total = left_recv[0].astype(F32)
    for i in range(1, ND):
        total = total + left_recv[i].astype(F32)
    left_out[...] = total.astype(BF16)
    lg_all[d] = left_out[...]
    start_all(lg_copy)
    for s in range(top - 1):
        for q in range(NQ):
            term(s, q).wait_recv()
        iacc[...] += chain_in[s].astype(F32)
    for q in range(NQ):
        term(top - 1, q).wait_recv()
        rows = rows_of(q)
        ig_v[rows] = (iacc[rows] + chain_in[top - 1, rows].astype(F32)).astype(BF16)
    stores.append(pltpu.make_async_copy(ig_v, ig_h, local.at[9]))
    stores[-1].start()
    receive_all(rg_copy)
    stores.append(pltpu.make_async_copy(rg_all, rg_h, local.at[7]))
    stores[-1].start()
    for ph in range(2):
        for copy in (ar_core, ar_y, ag_y, ag_core):
            copy(ph).wait_send()
        for k in range(2):
            near_tap(ph, k).wait_send()

        @pl.loop(1, Z)
        def _(k):
            z_scatter(ph, k).wait_send()
            z_gather(ph, k).wait_send()

    @pl.loop(1, ND)
    def _(k):
        for copy in (wg_first, wg_second, rg_copy, ls_copy):
            copy(k).wait_send()

    for q in range(NQ):
        for s in range(top):
            z_tap(s, q).wait_send()
        z_pass(q).wait_send()
        for s in range(nz):
            term(s, q).wait_send()

    receive_all(lg_copy)
    stores.append(pltpu.make_async_copy(lg_all, lg_h, local.at[8]))
    stores[-1].start()

    @pl.loop(1, ND)
    def _(k):
        lg_copy(k).wait_send()

    for store in stores:
        store.wait()


def hand_over(*refs):
    n = (len(refs) - 1) // 3
    ins, outs, held, sems = refs[:n], refs[n : 2 * n], refs[2 * n : 3 * n], refs[-1]
    load = [pltpu.make_async_copy(ins[i], held[i], sems.at[0, i]) for i in range(n)]
    store = [pltpu.make_async_copy(held[i], outs[i], sems.at[1, i]) for i in range(n)]
    for copy in load:
        copy.start()
    for i in range(n):
        load[i].wait()
        store[i].start()
    for copy in store:
        copy.wait()


def on_device(tokens, block_weight, left_factor, right_factor, out_cotangent):
    ND = lax.axis_size("dp")
    Z = lax.axis_size("mp") // 4
    T, C = tokens.shape
    K, _, H = block_weight.shape
    R = right_factor.shape[0]
    RB = C // ND
    any_spec = pl.BlockSpec(memory_space=pl.ANY)
    bf = lambda *shape: pltpu.VMEM(shape, BF16)
    fl = lambda *shape: pltpu.VMEM(shape, F32)
    dma = lambda *shape: pltpu.SemaphoreType.DMA(shape)
    out = lambda *shape: jax.ShapeDtypeStruct(shape, BF16)
    act, ig, wg, lg, rg = pl.pallas_call(
        functools.partial(kernel, Z, ND),
        out_shape=(out(T, H), out(T, C), out(K, RB, H), out(ND, RB, R), out(ND, RB, H)),
        in_specs=[any_spec] * 5,
        out_specs=[any_spec] * 5,
        scratch_shapes=[
            bf(T, C), bf(K, C, H), bf(C, R), bf(R, H), bf(T, H),
            fl(T, H), bf(T, H), bf(T, H),
            fl(2, 2, T // 2, R), fl(2, T // 2, R), fl(2, 2, T // 4, R), bf(2, 2, T // 4, R), bf(2, T // 4, R),
            bf(2, Z, 16, 128), bf(2, Z, 16, 128), bf(2, 2, 2, Z, 16, 128), bf(2, T, R),
            bf(K - 1, T, C), bf(2, T, C), bf(2, T, C),
            fl(T, C), bf(K - 3, T, C), bf(K - 3, T, C), fl(T, C), bf(T, C),
            bf(ND, K + 1, RB, H), bf(ND, K + 1, RB, H), bf(K + 1, RB, H), bf(ND, RB, H),
            bf(ND, RB, R), bf(ND, RB, R), bf(RB, R), bf(ND, RB, R),
            dma(2, 6), dma(2, 6), dma(2, 2, Z), dma(2, 2, Z),
            dma(K - 3, NQ), dma(K - 3, NQ), dma(K - 3, NQ), dma(K - 3, NQ),
            dma(5, ND), dma(5, ND), dma(10),
        ],
        compiler_params=pltpu.CompilerParams(
            collective_id=0, has_side_effects=True, vmem_limit_bytes=56 * 1024 * 1024
        ),
    )(tokens, block_weight, left_factor, right_factor, out_cotangent)
    results = (act, ig, wg, lg, rg)
    act, ig, wg, lg, rg = pl.pallas_call(
        hand_over,
        out_shape=tuple(out(*x.shape) for x in results),
        in_specs=[any_spec] * 5,
        out_specs=[any_spec] * 5,
        scratch_shapes=[bf(*x.shape) for x in results] + [dma(2, 5)],
    )(*results)
    return act, ig, wg, lg.reshape(C, R), rg.reshape(R, H)


def solution(mesh):
    return jax.shard_map(
        on_device,
        mesh=mesh,
        in_specs=(P("dp", "mp"), P(None, None, "mp"), P("mp", None), P(None, "mp"), P("dp", "mp")),
        out_specs=(P("dp", "mp"), P("dp", "mp"), P(None, "dp", "mp"), P("mp", None), P(None, "mp")),
        check_vma=False,
    )
```

```python
import functools

import jax
import jax.numpy as jnp
from jax import lax
from jax.experimental import pallas as pl
from jax.experimental.pallas import tpu as pltpu
from jax.sharding import PartitionSpec as P

gelu_scale = 0.7978845608028654
gelu_cubic = 0.044715
F32 = jnp.float32
BF16 = jnp.bfloat16

AR_CORE, AR_Y, TAP_CORE, TAP_Y = range(4)
NQ = 4


def gelu_parts(preact):
    inner = gelu_scale * (preact + gelu_cubic * preact * preact * preact)
    tangent = jnp.tanh(inner)
    value = 0.5 * preact * (1.0 + tangent)
    slope = 0.5 * (1.0 + tangent) + 0.5 * preact * (1.0 - tangent * tangent) * gelu_scale * (
        1.0 + 3.0 * gelu_cubic * preact * preact
    )
    return value, slope


def mm(a, b):
    return lax.dot_general(a, b, (((1,), (0,)), ((), ())), preferred_element_type=F32)


def mm_nt(a, b):
    return lax.dot_general(a, b, (((1,), (1,)), ((), ())), preferred_element_type=F32)


def mm_tn(a, b):
    return lax.dot_general(a, b, (((0,), (0,)), ((), ())), preferred_element_type=F32)


def kernel(
    Z, ND,
    tok_h, w_h, left_h, right_h, cot_h,
    act_h, ig_h, wg_h, lg_h, rg_h,
    tok_v, w_v, left_v, right_v, cot_v,
    acc, act_v, gp_v,
    part, rx_core, half, half_send, rx_y, z_send, z_recv, gathered, lat,
    taps, near_out, near_in, own, chain_out, chain_in, iacc, ig_v,
    wg_send, wg_recv, wg_out, rg_all, left_send, left_recv, left_out, lg_all,
    one_send, one_recv, zs_send, zs_recv, g_send, g_recv, f_send, f_recv, b_send, b_recv, d_send, d_recv, local,
):
    T, C = tok_v.shape
    R, H = right_v.shape
    K = w_v.shape[0]
    T2, T4, TQ = T // 2, T // 4, T // NQ
    RB = C // ND
    NC = R // 128
    nz = K - 3
    top = nz - 1

    d = lax.axis_index("dp")
    m = lax.axis_index("mp")
    c = lax.rem(m, 2)
    y = lax.rem(lax.div(m, 2), 2)
    z = lax.div(m, 4)
    base = m - z * 4

    def flip(stride):
        return m + stride - 2 * stride * lax.rem(lax.div(m, stride), 2)

    def z_at(k):
        return base + 4 * lax.rem(z + k, Z)

    def by_distance(i):
        odd = lax.rem(i, 2)
        return odd * lax.div(i + 1, 2) + (1 - odd) * (Z - lax.div(i, 2))

    core_peer, y_peer = flip(1), flip(2)

    def to(src, dst, send, recv, **where):
        return pltpu.make_async_remote_copy(
            src_ref=src, dst_ref=dst, send_sem=send, recv_sem=recv,
            device_id=where, device_id_type=pl.DeviceIdType.MESH,
        )

    def one(ph, k, src, dst, peer):
        return to(src, dst, one_send.at[ph, k], one_recv.at[ph, k], mp=peer)

    barrier = pltpu.get_barrier_semaphore()

    def greet(**where):
        pl.semaphore_signal(barrier, inc=1, device_id=where, device_id_type=pl.DeviceIdType.MESH)

    @pl.loop(1, Z)
    def _(k):
        greet(mp=z_at(k))

    @pl.loop(1, ND)
    def _(k):
        greet(dp=lax.rem(d + k, ND))

    greet(mp=core_peer)
    greet(mp=y_peer)

    loads = [
        pltpu.make_async_copy(src, dst, local.at[i])
        for i, (src, dst) in enumerate(
            [(tok_h, tok_v), (left_h, left_v), (w_h, w_v), (right_h, right_v), (cot_h, cot_v)]
        )
    ]
    for load in loads:
        load.start()

    def ar_core(ph):
        return one(ph, AR_CORE, part.at[ph, 1 - c], rx_core.at[ph], core_peer)

    def ar_y(ph):
        return one(ph, AR_Y, half_send.at[ph, 1 - y], rx_y.at[ph], y_peer)

    def ag_y(ph, p, incoming=False):
        piece = gathered.at[ph, c, 1 - y if incoming else y, p]
        return to(piece, piece, g_send.at[ph, 0, p], g_recv.at[ph, 0, p], mp=y_peer)

    def ag_core(ph, own_y, p, incoming=False):
        piece = gathered.at[ph, 1 - c if incoming else c, y if own_y else 1 - y, p]
        row = 1 if own_y else 2
        return to(piece, piece, g_send.at[ph, row, p], g_recv.at[ph, row, p], mp=core_peer)

    def z_scatter(ph, k):
        there = lax.rem(z + k, Z)
        return to(
            z_send.at[ph, there], z_recv.at[ph, z], zs_send.at[ph, 0, there], zs_recv.at[ph, 0, z],
            mp=z_at(k),
        )

    def z_scatter_in(ph, k):
        there = lax.rem(z + k, Z)
        return to(
            z_send.at[ph, there], z_recv.at[ph, there], zs_send.at[ph, 0, there],
            zs_recv.at[ph, 0, there], mp=z_at(k),
        )

    def z_gather(ph, k):
        there = lax.rem(z + k, Z)
        return to(
            gathered.at[ph, c, y, z], gathered.at[ph, c, y, z], zs_send.at[ph, 1, there],
            zs_recv.at[ph, 1, z], mp=z_at(k),
        )

    def z_gather_in(ph, k):
        there = lax.rem(z + k, Z)
        return to(
            gathered.at[ph, c, y, there], gathered.at[ph, c, y, there], zs_send.at[ph, 1, there],
            zs_recv.at[ph, 1, there], mp=z_at(k),
        )

    def near_tap(ph, k):
        src = tok_h if ph == 0 else near_out.at[k]
        dst = taps.at[k] if ph == 0 else near_in.at[k]
        return one(ph, TAP_CORE + k, src, dst, flip(1 << k))

    def rows_of(q):
        return pl.ds(q * TQ, TQ)

    def z_flip(at, k):
        return at + (1 << k) - (2 << k) * lax.rem(lax.div(at, 1 << k), 2)

    def way(at, k):
        return lax.rem(lax.div(at, 1 << k), 2)

    onward = z_flip(z_flip(z, top - 1), top)

    def z_tap(s, q):
        return to(
            tok_h.at[rows_of(q)], taps.at[2 + s, rows_of(q)], f_send.at[s, q], f_recv.at[s, q],
            mp=base + 4 * z_flip(z, s),
        )

    def z_pass(q):
        return to(
            taps.at[1 + top, rows_of(q)], taps.at[2 + top, rows_of(q)], f_send.at[top, q],
            f_recv.at[top, q], mp=base + 4 * onward,
        )

    def pass_on(q):
        z_tap(top - 1, q).wait_recv()
        z_pass(q).start()

    def arrived(s, q):
        (z_pass(q) if s == top else z_tap(s, q)).wait_recv()

    def term(s, q):
        peer = onward if s == top else z_flip(z, s)
        return to(
            chain_out.at[s, rows_of(q)], chain_in.at[s, rows_of(q)], b_send.at[s, q],
            b_recv.at[s, q], mp=base + 4 * peer,
        )

    def add_on(q):
        term(top, q).wait_recv()
        rows = rows_of(q)
        chain_out[top - 1, rows] = (own[rows] + chain_in[top, rows].astype(F32)).astype(BF16)
        term(top - 1, q).start()

    def after_core(ph):
        ar_core(ph).wait_recv()
        for i in range(2):
            rows = pl.ds(i * T4, T4)
            both = part[ph, c, rows] + rx_core[ph, rows]
            half[ph, i] = both
            half_send[ph, i] = both.astype(BF16)
        ar_y(ph).start()

    def after_y(ph):
        ar_y(ph).wait_recv()
        for rb in range(T4 // 16):
            rows = pl.ds(rb * 16, 16)
            total = (half[ph, y, rows] + rx_y[ph, rows].astype(F32)).astype(BF16)
            for ch in range(NC):
                z_send[ph, rb * NC + ch] = total[:, ch * 128 : (ch + 1) * 128]
        z_recv[ph, z] = z_send[ph, z]

        @pl.loop(1, Z)
        def _(k):
            z_scatter(ph, by_distance(Z - k)).start()

    def after_scatter(ph):
        @pl.loop(1, Z)
        def _(k):
            z_scatter_in(ph, k).wait_recv()

        total = z_recv[ph, 0].astype(F32)
        for i in range(1, Z):
            total = total + z_recv[ph, i].astype(F32)
        gathered[ph, c, y, z] = total.astype(BF16)

        @pl.loop(1, Z)
        def _(k):
            z_gather(ph, by_distance(Z - k)).start()

    def piece_at(i):
        return lax.rem(z + by_distance(i), Z)

    def after_gather(ph):
        ag_y(ph, z).start()
        ag_core(ph, True, z).start()

        @pl.loop(1, Z)
        def _(i):
            z_gather_in(ph, by_distance(i)).wait_recv()
            ag_y(ph, piece_at(i)).start()
            ag_core(ph, True, piece_at(i)).start()

    def after_gather_y(ph):
        def onward_core(p):
            ag_y(ph, p, True).wait_recv()
            ag_core(ph, False, p).start()

        onward_core(z)

        @pl.loop(1, Z)
        def _(i):
            onward_core(piece_at(i))

    def after_gather_core(ph):
        @pl.loop(0, Z)
        def _(p):
            ag_core(ph, True, p, True).wait_recv()
            ag_core(ph, False, p, True).wait_recv()

        for i in range(2):
            for j in range(2):
                for rb in range(T4 // 16):
                    for ch in range(NC):
                        lat[ph, pl.ds(i * T2 + j * T4 + rb * 16, 16), pl.ds(ch * 128, 128)] = (
                            gathered[ph, i, j, rb * NC + ch]
                        )

    loads[0].wait()
    loads[1].wait()
    partial = mm(tok_v[...], left_v[...])
    part[0, 0] = partial[:T2]
    part[0, 1] = partial[T2:]
    pl.semaphore_wait(barrier, Z - 1 + ND - 1 + 2)
    ar_core(0).start()
    z_tap(top - 1, 0).start()
    for q in range(2):
        z_tap(0, q).start()
    after_core(0)
    near_tap(0, 0).start()
    loads[2].wait()
    acc[...] = mm(tok_v[...], w_v[0])
    after_y(0)
    z_tap(top - 1, 1).start()
    for q in range(2, NQ):
        z_tap(0, q).start()
    near_tap(0, 1).start()
    pass_on(0)
    after_scatter(0)
    for q in range(2, NQ):
        z_tap(top - 1, q).start()
    pass_on(1)
    for k in range(2):
        near_tap(0, k).wait_recv()
        acc[...] += mm(taps[k], w_v[1 + k])
    pass_on(2)
    for q in range(NQ):
        for s in range(1, top - 1):
            z_tap(s, q).start()
    pass_on(3)
    after_gather(0)
    loads[3].wait()
    loads[4].wait()
    after_gather_y(0)
    acc[...] += mm(taps[1 + top], w_v[2 + top])
    for q in range(NQ):
        arrived(0, q)
    acc[...] += mm(taps[2], w_v[3])
    after_gather_core(0)
    acc[...] += mm(lat[0], right_v[...])

    stores = []
    for q in range(NQ):
        rows = rows_of(q)
        for s in range(1, top - 1):
            arrived(s, q)
            acc[rows] += mm(taps[2 + s, rows], w_v[3 + s])
        arrived(top, q)
        acc[rows] += mm(taps[2 + top, rows], w_v[3 + top])

        @pl.loop(0, TQ // 32)
        def _(i):
            here = pl.ds(pl.multiple_of(q * TQ + i * 32, 32), 32)
            value, slope = gelu_parts(acc[here])
            act_v[here] = value.astype(BF16)
            gp_v[here] = (cot_v[here].astype(F32) * slope).astype(BF16)

        chain_out[top, rows] = mm_nt(gp_v[rows], w_v[3 + top]).astype(BF16)
        if q == 0:
            term(top, q).start()

    stores = [pltpu.make_async_copy(act_v, act_h, local.at[5])]
    stores[0].start()
    partial = mm_nt(gp_v[...], right_v[...])
    part[1, 0] = partial[:T2]
    part[1, 1] = partial[T2:]
    ar_core(1).start()

    def fill(s):
        chain_out[s] = mm_nt(gp_v[...], w_v[3 + s]).astype(BF16)

    def fill_near(k):
        near_out[k] = mm_nt(gp_v[...], w_v[1 + k]).astype(BF16)

    def fill_weight(t):
        if t == K:
            source = lat[0]
        elif t == 0:
            source = tok_v[...]
        else:
            source = taps[t - 1]
        wg_send[:, t] = mm_tn(source, gp_v[...]).astype(BF16).reshape(ND, RB, H)

    def dp_copy(row, k, src, dst, incoming):
        there = lax.rem(d + k, ND)
        return to(
            src(there), dst(there if incoming else d), d_send.at[row, there],
            d_recv.at[row, there if incoming else d], dp=there,
        )

    KH = (K + 1) // 2

    def wg_copy(part_no, k, incoming=False):
        planes = pl.ds(0, KH) if part_no == 0 else pl.ds(KH, K + 1 - KH)
        return dp_copy(
            4 * part_no, k, lambda p: wg_send.at[p, planes], lambda p: wg_recv.at[p, planes], incoming
        )

    wg_first = functools.partial(wg_copy, 0)
    wg_second = functools.partial(wg_copy, 1)

    def rg_copy(k, incoming=False):
        return dp_copy(1, k, lambda p: wg_out.at[K], lambda p: rg_all.at[p], incoming)

    def ls_copy(k, incoming=False):
        return dp_copy(2, k, lambda p: left_send.at[p], lambda p: left_recv.at[p], incoming)

    def lg_copy(k, incoming=False):
        return dp_copy(3, k, lambda p: left_out, lambda p: lg_all.at[p], incoming)

    def start_all(make):
        @pl.loop(1, ND)
        def _(k):
            make(k).start()

    def receive_all(make):
        @pl.loop(1, ND)
        def _(k):
            make(k, True).wait_recv()

    own[...] = mm_nt(gp_v[...], w_v[2 + top])
    after_core(1)
    fill_near(0)
    near_tap(1, 0).start()
    fill_near(1)
    for s in range(top - 1):
        fill(s)
    for t in range(2):
        fill_weight(t)
    after_y(1)
    term(top, 1).start()
    for q in range(NQ):
        term(0, q).start()
    near_tap(1, 1).start()
    for t in range(2, KH):
        fill_weight(t)
    start_all(wg_first)
    add_on(0)
    for t in range(KH, K + 1):
        fill_weight(t)
    start_all(wg_second)
    wg_recv[d] = wg_send[d]
    iacc[...] = mm_nt(gp_v[...], w_v[0])
    after_scatter(1)
    for q in range(2, NQ):
        term(top, q).start()
    add_on(1)
    add_on(2)
    for q in range(NQ):
        for s in range(1, top - 1):
            term(s, q).start()
    add_on(3)
    after_gather(1)
    after_gather_y(1)
    after_gather_core(1)
    left_send[...] = mm_tn(tok_v[...], lat[1]).astype(BF16).reshape(ND, RB, R)
    left_recv[d] = left_send[d]
    start_all(ls_copy)
    iacc[...] += mm_nt(lat[1], left_v[...])
    receive_all(wg_first)
    receive_all(wg_second)

    @pl.loop(0, K + 1)
    def _(t):
        total = wg_recv[0, t].astype(F32)
        for i in range(1, ND):
            total = total + wg_recv[i, t].astype(F32)
        wg_out[t] = total.astype(BF16)

    rg_all[d] = wg_out[K]
    start_all(rg_copy)
    stores.append(pltpu.make_async_copy(wg_out.at[pl.ds(0, K)], wg_h, local.at[6]))
    stores[-1].start()
    receive_all(ls_copy)
    total = left_recv[0].astype(F32)
    for i in range(1, ND):
        total = total + left_recv[i].astype(F32)
    left_out[...] = total.astype(BF16)
    lg_all[d] = left_out[...]
    start_all(lg_copy)
    for k in range(2):
        near_tap(1, k).wait_recv()
        iacc[...] += near_in[k].astype(F32)
    for s in range(top - 1):
        for q in range(NQ):
            term(s, q).wait_recv()
        iacc[...] += chain_in[s].astype(F32)
    for q in range(NQ):
        term(top - 1, q).wait_recv()
        rows = rows_of(q)
        ig_v[rows] = (iacc[rows] + chain_in[top - 1, rows].astype(F32)).astype(BF16)
    stores.append(pltpu.make_async_copy(ig_v, ig_h, local.at[9]))
    stores[-1].start()
    receive_all(rg_copy)
    stores.append(pltpu.make_async_copy(rg_all, rg_h, local.at[7]))
    stores[-1].start()
    for ph in range(2):
        for copy in (ar_core, ar_y):
            copy(ph).wait_send()
        for k in range(2):
            near_tap(ph, k).wait_send()

        @pl.loop(1, Z)
        def _(k):
            z_scatter(ph, k).wait_send()
            z_gather(ph, k).wait_send()

        @pl.loop(0, Z)
        def _(p):
            ag_y(ph, p).wait_send()
            ag_core(ph, True, p).wait_send()
            ag_core(ph, False, p).wait_send()

    @pl.loop(1, ND)
    def _(k):
        for copy in (wg_first, wg_second, rg_copy, ls_copy):
            copy(k).wait_send()

    for q in range(NQ):
        for s in range(top):
            z_tap(s, q).wait_send()
        z_pass(q).wait_send()
        for s in range(nz):
            term(s, q).wait_send()

    receive_all(lg_copy)
    stores.append(pltpu.make_async_copy(lg_all, lg_h, local.at[8]))
    stores[-1].start()

    @pl.loop(1, ND)
    def _(k):
        lg_copy(k).wait_send()

    for store in stores:
        store.wait()


def hand_over(*refs):
    n = len(refs) // 2
    sems = refs[-1]
    store = [pltpu.make_async_copy(refs[i], refs[n + i], sems.at[i]) for i in range(n)]
    for copy in store:
        copy.start()
    for copy in store:
        copy.wait()


def on_device(tokens, block_weight, left_factor, right_factor, out_cotangent):
    ND = lax.axis_size("dp")
    Z = lax.axis_size("mp") // 4
    T, C = tokens.shape
    K, _, H = block_weight.shape
    R = right_factor.shape[0]
    RB = C // ND
    any_spec = pl.BlockSpec(memory_space=pl.ANY)
    bf = lambda *shape: pltpu.VMEM(shape, BF16)
    fl = lambda *shape: pltpu.VMEM(shape, F32)
    dma = lambda *shape: pltpu.SemaphoreType.DMA(shape)
    out = lambda *shape: jax.ShapeDtypeStruct(shape, BF16)
    act, ig, wg, lg, rg = pl.pallas_call(
        functools.partial(kernel, Z, ND),
        out_shape=(out(T, H), out(T, C), out(K, RB, H), out(ND, RB, R), out(ND, RB, H)),
        in_specs=[pl.BlockSpec(memory_space=pltpu.HBM)] * 5,
        out_specs=[any_spec] * 5,
        scratch_shapes=[
            bf(T, C), bf(K, C, H), bf(C, R), bf(R, H), bf(T, H),
            fl(T, H), bf(T, H), bf(T, H),
            fl(2, 2, T // 2, R), fl(2, T // 2, R), fl(2, 2, T // 4, R), bf(2, 2, T // 4, R), bf(2, T // 4, R),
            bf(2, Z, 16, 128), bf(2, Z, 16, 128), bf(2, 2, 2, Z, 16, 128), bf(2, T, R),
            bf(K - 1, T, C), bf(2, T, C), bf(2, T, C),
            fl(T, C), bf(K - 3, T, C), bf(K - 3, T, C), fl(T, C), bf(T, C),
            bf(ND, K + 1, RB, H), bf(ND, K + 1, RB, H), bf(K + 1, RB, H), bf(ND, RB, H),
            bf(ND, RB, R), bf(ND, RB, R), bf(RB, R), bf(ND, RB, R),
            dma(2, 4), dma(2, 4), dma(2, 2, Z), dma(2, 2, Z), dma(2, 3, Z), dma(2, 3, Z),
            dma(K - 3, NQ), dma(K - 3, NQ), dma(K - 3, NQ), dma(K - 3, NQ),
            dma(5, ND), dma(5, ND), dma(10),
        ],
        compiler_params=pltpu.CompilerParams(
            collective_id=0, has_side_effects=True, vmem_limit_bytes=26 * 1024 * 1024
        ),
    )(*[pltpu.with_memory_space_constraint(v, pltpu.HBM) for v in (tokens, block_weight, left_factor, right_factor, out_cotangent)])
    results = (act, ig, wg, lg, rg)
    act, ig, wg, lg, rg = pl.pallas_call(
        hand_over,
        out_shape=tuple(out(*x.shape) for x in results),
        in_specs=[pl.BlockSpec(memory_space=pltpu.VMEM)] * 5,
        out_specs=[pl.BlockSpec(memory_space=pltpu.HBM)] * 5,
        scratch_shapes=[dma(5)],
        compiler_params=pltpu.CompilerParams(vmem_limit_bytes=4 * 1024 * 1024),
    )(*results)
    return act, ig, wg, lg.reshape(C, R), rg.reshape(R, H)


def solution(mesh):
    return jax.shard_map(
        on_device,
        mesh=mesh,
        in_specs=(P("dp", "mp"), P(None, None, "mp"), P("mp", None), P(None, "mp"), P("dp", "mp")),
        out_specs=(P("dp", "mp"), P("dp", "mp"), P(None, "dp", "mp"), P("mp", None), P(None, "mp")),
        check_vma=False,
    )
```

```python
import functools

import jax
import jax.numpy as jnp
from jax import lax
from jax.experimental import pallas as pl
from jax.experimental.pallas import tpu as pltpu
from jax.sharding import PartitionSpec as P

gelu_scale = 0.7978845608028654
gelu_cubic = 0.044715
F32 = jnp.float32
BF16 = jnp.bfloat16

AR_CORE, AR_Y, TAP_CORE, TAP_Y = range(4)
NQ = 4


def gelu_parts(preact):
    inner = gelu_scale * (preact + gelu_cubic * preact * preact * preact)
    tangent = jnp.tanh(inner)
    value = 0.5 * preact * (1.0 + tangent)
    slope = 0.5 * (1.0 + tangent) + 0.5 * preact * (1.0 - tangent * tangent) * gelu_scale * (
        1.0 + 3.0 * gelu_cubic * preact * preact
    )
    return value, slope


def mm(a, b):
    return lax.dot_general(a, b, (((1,), (0,)), ((), ())), preferred_element_type=F32)


def mm_nt(a, b):
    return lax.dot_general(a, b, (((1,), (1,)), ((), ())), preferred_element_type=F32)


def mm_tn(a, b):
    return lax.dot_general(a, b, (((0,), (0,)), ((), ())), preferred_element_type=F32)


def kernel(
    Z, ND,
    tok_h, w_h, left_h, right_h, cot_h,
    act_h, ig_h, wg_h, lg_h, rg_h,
    tok_v, w_v, left_v, right_v, cot_v,
    acc, act_v, gp_v,
    part, rx_core, half, half_send, rx_y, z_send, z_recv, gathered, lat,
    taps, near_out, near_in, own, chain_out, chain_in, iacc, ig_v,
    wg_send, wg_recv, wg_out, rg_all, left_send, left_recv, left_out, lg_all,
    one_send, one_recv, zs_send, zs_recv, g_send, g_recv, f_send, f_recv, b_send, b_recv, d_send, d_recv, local,
):
    T, C = tok_v.shape
    R, H = right_v.shape
    K = w_v.shape[0]
    T2, T4, TQ = T // 2, T // 4, T // NQ
    RB = C // ND
    NC = R // 128
    nz = K - 3
    top = nz - 1

    d = lax.axis_index("dp")
    m = lax.axis_index("mp")
    c = lax.rem(m, 2)
    y = lax.rem(lax.div(m, 2), 2)
    z = lax.div(m, 4)
    base = m - z * 4

    def flip(stride):
        return m + stride - 2 * stride * lax.rem(lax.div(m, stride), 2)

    def z_at(k):
        return base + 4 * lax.rem(z + k, Z)

    def by_distance(i):
        odd = lax.rem(i, 2)
        return odd * lax.div(i + 1, 2) + (1 - odd) * (Z - lax.div(i, 2))

    core_peer, y_peer = flip(1), flip(2)

    def to(src, dst, send, recv, **where):
        return pltpu.make_async_remote_copy(
            src_ref=src, dst_ref=dst, send_sem=send, recv_sem=recv,
            device_id=where, device_id_type=pl.DeviceIdType.MESH,
        )

    def one(ph, k, src, dst, peer):
        return to(src, dst, one_send.at[ph, k], one_recv.at[ph, k], mp=peer)

    barrier = pltpu.get_barrier_semaphore()

    def greet(**where):
        pl.semaphore_signal(barrier, inc=1, device_id=where, device_id_type=pl.DeviceIdType.MESH)

    @pl.loop(1, Z)
    def _(k):
        greet(mp=z_at(k))

    @pl.loop(1, ND)
    def _(k):
        greet(dp=lax.rem(d + k, ND))

    greet(mp=core_peer)
    greet(mp=y_peer)

    loads = [
        pltpu.make_async_copy(src, dst, local.at[i])
        for i, (src, dst) in enumerate(
            [(tok_h, tok_v), (left_h, left_v), (w_h, w_v), (right_h, right_v), (cot_h, cot_v)]
        )
    ]
    for load in loads:
        load.start()

    def ar_core(ph):
        return one(ph, AR_CORE, part.at[ph, 1 - c], rx_core.at[ph], core_peer)

    def ar_y(ph):
        return one(ph, AR_Y, half_send.at[ph, 1 - y], rx_y.at[ph], y_peer)

    def ag_y(ph, p, incoming=False):
        piece = gathered.at[ph, c, 1 - y if incoming else y, p]
        return to(piece, piece, g_send.at[ph, 0, p], g_recv.at[ph, 0, p], mp=y_peer)

    def ag_core(ph, own_y, p, incoming=False):
        piece = gathered.at[ph, 1 - c if incoming else c, y if own_y else 1 - y, p]
        row = 1 if own_y else 2
        return to(piece, piece, g_send.at[ph, row, p], g_recv.at[ph, row, p], mp=core_peer)

    def z_scatter(ph, k):
        there = lax.rem(z + k, Z)
        return to(
            z_send.at[ph, there], z_recv.at[ph, z], zs_send.at[ph, 0, there], zs_recv.at[ph, 0, z],
            mp=z_at(k),
        )

    def z_scatter_in(ph, k):
        there = lax.rem(z + k, Z)
        return to(
            z_send.at[ph, there], z_recv.at[ph, there], zs_send.at[ph, 0, there],
            zs_recv.at[ph, 0, there], mp=z_at(k),
        )

    def z_gather(ph, k):
        there = lax.rem(z + k, Z)
        return to(
            gathered.at[ph, c, y, z], gathered.at[ph, c, y, z], zs_send.at[ph, 1, there],
            zs_recv.at[ph, 1, z], mp=z_at(k),
        )

    def z_gather_in(ph, k):
        there = lax.rem(z + k, Z)
        return to(
            gathered.at[ph, c, y, there], gathered.at[ph, c, y, there], zs_send.at[ph, 1, there],
            zs_recv.at[ph, 1, there], mp=z_at(k),
        )

    def near_tap(ph, k):
        src = tok_h if ph == 0 else near_out.at[k]
        dst = taps.at[k] if ph == 0 else near_in.at[k]
        return one(ph, TAP_CORE + k, src, dst, flip(1 << k))

    def rows_of(q):
        return pl.ds(q * TQ, TQ)

    def z_flip(at, k):
        return at + (1 << k) - (2 << k) * lax.rem(lax.div(at, 1 << k), 2)

    def way(at, k):
        return lax.rem(lax.div(at, 1 << k), 2)

    onward = z_flip(z_flip(z, top - 1), top)

    def z_tap(s, q):
        return to(
            tok_h.at[rows_of(q)], taps.at[2 + s, rows_of(q)], f_send.at[s, q], f_recv.at[s, q],
            mp=base + 4 * z_flip(z, s),
        )

    def z_pass(q):
        return to(
            taps.at[1 + top, rows_of(q)], taps.at[2 + top, rows_of(q)], f_send.at[top, q],
            f_recv.at[top, q], mp=base + 4 * onward,
        )

    def pass_on(q):
        z_tap(top - 1, q).wait_recv()
        z_pass(q).start()

    def arrived(s, q):
        (z_pass(q) if s == top else z_tap(s, q)).wait_recv()

    def term(s, q):
        peer = onward if s == top else z_flip(z, s)
        return to(
            chain_out.at[s, rows_of(q)], chain_in.at[s, rows_of(q)], b_send.at[s, q],
            b_recv.at[s, q], mp=base + 4 * peer,
        )

    def add_on(q):
        term(top, q).wait_recv()
        rows = rows_of(q)
        chain_out[top - 1, rows] = (own[rows] + chain_in[top, rows].astype(F32)).astype(BF16)
        term(top - 1, q).start()

    def after_core(ph):
        ar_core(ph).wait_recv()
        for i in range(2):
            rows = pl.ds(i * T4, T4)
            both = part[ph, c, rows] + rx_core[ph, rows]
            half[ph, i] = both
            half_send[ph, i] = both.astype(BF16)
        ar_y(ph).start()

    def after_y(ph):
        ar_y(ph).wait_recv()
        for rb in range(T4 // 16):
            rows = pl.ds(rb * 16, 16)
            total = (half[ph, y, rows] + rx_y[ph, rows].astype(F32)).astype(BF16)
            for ch in range(NC):
                z_send[ph, rb * NC + ch] = total[:, ch * 128 : (ch + 1) * 128]
        z_recv[ph, z] = z_send[ph, z]

        @pl.loop(1, Z)
        def _(k):
            z_scatter(ph, by_distance(Z - k)).start()

    def after_scatter(ph):
        @pl.loop(1, Z)
        def _(k):
            z_scatter_in(ph, k).wait_recv()

        total = z_recv[ph, 0].astype(F32)
        for i in range(1, Z):
            total = total + z_recv[ph, i].astype(F32)
        gathered[ph, c, y, z] = total.astype(BF16)

        @pl.loop(1, Z)
        def _(k):
            z_gather(ph, by_distance(Z - k)).start()

    def piece_at(i):
        return lax.rem(z + by_distance(i), Z)

    def after_gather(ph):
        ag_y(ph, z).start()
        ag_core(ph, True, z).start()

        @pl.loop(1, Z)
        def _(i):
            z_gather_in(ph, by_distance(i)).wait_recv()
            ag_y(ph, piece_at(i)).start()
            ag_core(ph, True, piece_at(i)).start()

    def after_gather_y(ph):
        def onward_core(p):
            ag_y(ph, p, True).wait_recv()
            ag_core(ph, False, p).start()

        onward_core(z)

        @pl.loop(1, Z)
        def _(i):
            onward_core(piece_at(i))

    def after_gather_core(ph):
        @pl.loop(0, Z)
        def _(p):
            ag_core(ph, True, p, True).wait_recv()
            ag_core(ph, False, p, True).wait_recv()

        for i in range(2):
            for j in range(2):
                for rb in range(T4 // 16):
                    for ch in range(NC):
                        lat[ph, pl.ds(i * T2 + j * T4 + rb * 16, 16), pl.ds(ch * 128, 128)] = (
                            gathered[ph, i, j, rb * NC + ch]
                        )

    pl.semaphore_wait(barrier, Z - 1 + ND - 1 + 2)
    z_tap(top - 1, 0).start()
    for q in range(2):
        z_tap(0, q).start()
    loads[0].wait()
    loads[1].wait()
    partial = mm(tok_v[...], left_v[...])
    part[0, 0] = partial[:T2]
    part[0, 1] = partial[T2:]
    ar_core(0).start()
    after_core(0)
    near_tap(0, 0).start()
    loads[2].wait()
    acc[...] = mm(tok_v[...], w_v[0])
    after_y(0)
    z_tap(top - 1, 1).start()
    for q in range(2, NQ):
        z_tap(0, q).start()
    near_tap(0, 1).start()
    pass_on(0)
    after_scatter(0)
    for q in range(2, NQ):
        z_tap(top - 1, q).start()
    pass_on(1)
    for k in range(2):
        near_tap(0, k).wait_recv()
        acc[...] += mm(taps[k], w_v[1 + k])
    pass_on(2)
    for q in range(NQ):
        for s in range(1, top - 1):
            z_tap(s, q).start()
    pass_on(3)
    after_gather(0)
    loads[3].wait()
    loads[4].wait()
    after_gather_y(0)
    acc[...] += mm(taps[1 + top], w_v[2 + top])
    for q in range(NQ):
        arrived(0, q)
    acc[...] += mm(taps[2], w_v[3])
    after_gather_core(0)
    acc[...] += mm(lat[0], right_v[...])

    stores = []
    for q in range(NQ):
        rows = rows_of(q)
        for s in range(1, top - 1):
            arrived(s, q)
            acc[rows] += mm(taps[2 + s, rows], w_v[3 + s])
        arrived(top, q)
        acc[rows] += mm(taps[2 + top, rows], w_v[3 + top])

        @pl.loop(0, TQ // 32)
        def _(i):
            here = pl.ds(pl.multiple_of(q * TQ + i * 32, 32), 32)
            value, slope = gelu_parts(acc[here])
            act_v[here] = value.astype(BF16)
            gp_v[here] = (cot_v[here].astype(F32) * slope).astype(BF16)

        chain_out[top, rows] = mm_nt(gp_v[rows], w_v[3 + top]).astype(BF16)
        if q == 0:
            term(top, q).start()

    stores = [pltpu.make_async_copy(act_v, act_h, local.at[5])]
    stores[0].start()
    partial = mm_nt(gp_v[...], right_v[...])
    part[1, 0] = partial[:T2]
    part[1, 1] = partial[T2:]
    ar_core(1).start()

    def fill(s):
        chain_out[s] = mm_nt(gp_v[...], w_v[3 + s]).astype(BF16)

    def fill_near(k):
        near_out[k] = mm_nt(gp_v[...], w_v[1 + k]).astype(BF16)

    def fill_weight(t):
        if t == K:
            source = lat[0]
        elif t == 0:
            source = tok_v[...]
        else:
            source = taps[t - 1]
        wg_send[:, t] = mm_tn(source, gp_v[...]).astype(BF16).reshape(ND, RB, H)

    def dp_copy(row, k, src, dst, incoming):
        there = lax.rem(d + k, ND)
        return to(
            src(there), dst(there if incoming else d), d_send.at[row, there],
            d_recv.at[row, there if incoming else d], dp=there,
        )

    KH = (K + 1) // 2

    def wg_copy(part_no, k, incoming=False):
        planes = pl.ds(0, KH) if part_no == 0 else pl.ds(KH, K + 1 - KH)
        return dp_copy(
            4 * part_no, k, lambda p: wg_send.at[p, planes], lambda p: wg_recv.at[p, planes], incoming
        )

    wg_first = functools.partial(wg_copy, 0)
    wg_second = functools.partial(wg_copy, 1)

    def rg_copy(k, incoming=False):
        return dp_copy(1, k, lambda p: wg_out.at[K], lambda p: rg_all.at[p], incoming)

    def ls_copy(k, incoming=False):
        return dp_copy(2, k, lambda p: left_send.at[p], lambda p: left_recv.at[p], incoming)

    def lg_copy(k, incoming=False):
        return dp_copy(3, k, lambda p: left_out, lambda p: lg_all.at[p], incoming)

    def start_all(make):
        @pl.loop(1, ND)
        def _(k):
            make(k).start()

    def receive_all(make):
        @pl.loop(1, ND)
        def _(k):
            make(k, True).wait_recv()

    own[...] = mm_nt(gp_v[...], w_v[2 + top])
    after_core(1)
    fill_near(0)
    near_tap(1, 0).start()
    fill_near(1)
    for s in range(top - 1):
        fill(s)
    for t in range(2):
        fill_weight(t)
    after_y(1)
    term(top, 1).start()
    for q in range(NQ):
        term(0, q).start()
    near_tap(1, 1).start()
    for t in range(2, KH):
        fill_weight(t)
    start_all(wg_first)
    add_on(0)
    for t in range(KH, K + 1):
        fill_weight(t)
    start_all(wg_second)
    wg_recv[d] = wg_send[d]
    iacc[...] = mm_nt(gp_v[...], w_v[0])
    after_scatter(1)
    for q in range(2, NQ):
        term(top, q).start()
    add_on(1)
    add_on(2)
    for q in range(NQ):
        for s in range(1, top - 1):
            term(s, q).start()
    add_on(3)
    after_gather(1)
    after_gather_y(1)
    after_gather_core(1)
    left_send[...] = mm_tn(tok_v[...], lat[1]).astype(BF16).reshape(ND, RB, R)
    left_recv[d] = left_send[d]
    start_all(ls_copy)
    iacc[...] += mm_nt(lat[1], left_v[...])
    receive_all(wg_first)
    receive_all(wg_second)

    @pl.loop(0, K + 1)
    def _(t):
        total = wg_recv[0, t].astype(F32)
        for i in range(1, ND):
            total = total + wg_recv[i, t].astype(F32)
        wg_out[t] = total.astype(BF16)

    rg_all[d] = wg_out[K]
    start_all(rg_copy)
    stores.append(pltpu.make_async_copy(wg_out.at[pl.ds(0, K)], wg_h, local.at[6]))
    stores[-1].start()
    receive_all(ls_copy)
    total = left_recv[0].astype(F32)
    for i in range(1, ND):
        total = total + left_recv[i].astype(F32)
    left_out[...] = total.astype(BF16)
    lg_all[d] = left_out[...]
    start_all(lg_copy)
    for k in range(2):
        near_tap(1, k).wait_recv()
        iacc[...] += near_in[k].astype(F32)
    for s in range(top - 1):
        for q in range(NQ):
            term(s, q).wait_recv()
        iacc[...] += chain_in[s].astype(F32)
    for q in range(NQ):
        term(top - 1, q).wait_recv()
        rows = rows_of(q)
        ig_v[rows] = (iacc[rows] + chain_in[top - 1, rows].astype(F32)).astype(BF16)
    stores.append(pltpu.make_async_copy(ig_v, ig_h, local.at[9]))
    stores[-1].start()
    receive_all(rg_copy)
    stores.append(pltpu.make_async_copy(rg_all, rg_h, local.at[7]))
    stores[-1].start()
    for ph in range(2):
        for copy in (ar_core, ar_y):
            copy(ph).wait_send()
        for k in range(2):
            near_tap(ph, k).wait_send()

        @pl.loop(1, Z)
        def _(k):
            z_scatter(ph, k).wait_send()
            z_gather(ph, k).wait_send()

        @pl.loop(0, Z)
        def _(p):
            ag_y(ph, p).wait_send()
            ag_core(ph, True, p).wait_send()
            ag_core(ph, False, p).wait_send()

    @pl.loop(1, ND)
    def _(k):
        for copy in (wg_first, wg_second, rg_copy, ls_copy):
            copy(k).wait_send()

    for q in range(NQ):
        for s in range(top):
            z_tap(s, q).wait_send()
        z_pass(q).wait_send()
        for s in range(nz):
            term(s, q).wait_send()

    receive_all(lg_copy)
    stores.append(pltpu.make_async_copy(lg_all, lg_h, local.at[8]))
    stores[-1].start()

    @pl.loop(1, ND)
    def _(k):
        lg_copy(k).wait_send()

    for store in stores:
        store.wait()


def hand_over(*refs):
    n = len(refs) // 2
    sems = refs[-1]
    store = [pltpu.make_async_copy(refs[i], refs[n + i], sems.at[i]) for i in range(n)]
    for copy in store:
        copy.start()
    for copy in store:
        copy.wait()


def on_device(tokens, block_weight, left_factor, right_factor, out_cotangent):
    ND = lax.axis_size("dp")
    Z = lax.axis_size("mp") // 4
    T, C = tokens.shape
    K, _, H = block_weight.shape
    R = right_factor.shape[0]
    RB = C // ND
    any_spec = pl.BlockSpec(memory_space=pl.ANY)
    bf = lambda *shape: pltpu.VMEM(shape, BF16)
    fl = lambda *shape: pltpu.VMEM(shape, F32)
    dma = lambda *shape: pltpu.SemaphoreType.DMA(shape)
    out = lambda *shape: jax.ShapeDtypeStruct(shape, BF16)
    act, ig, wg, lg, rg = pl.pallas_call(
        functools.partial(kernel, Z, ND),
        out_shape=(out(T, H), out(T, C), out(K, RB, H), out(ND, RB, R), out(ND, RB, H)),
        in_specs=[pl.BlockSpec(memory_space=pltpu.HBM)] * 5,
        out_specs=[any_spec] * 5,
        scratch_shapes=[
            bf(T, C), bf(K, C, H), bf(C, R), bf(R, H), bf(T, H),
            fl(T, H), bf(T, H), bf(T, H),
            fl(2, 2, T // 2, R), fl(2, T // 2, R), fl(2, 2, T // 4, R), bf(2, 2, T // 4, R), bf(2, T // 4, R),
            bf(2, Z, 16, 128), bf(2, Z, 16, 128), bf(2, 2, 2, Z, 16, 128), bf(2, T, R),
            bf(K - 1, T, C), bf(2, T, C), bf(2, T, C),
            fl(T, C), bf(K - 3, T, C), bf(K - 3, T, C), fl(T, C), bf(T, C),
            bf(ND, K + 1, RB, H), bf(ND, K + 1, RB, H), bf(K + 1, RB, H), bf(ND, RB, H),
            bf(ND, RB, R), bf(ND, RB, R), bf(RB, R), bf(ND, RB, R),
            dma(2, 4), dma(2, 4), dma(2, 2, Z), dma(2, 2, Z), dma(2, 3, Z), dma(2, 3, Z),
            dma(K - 3, NQ), dma(K - 3, NQ), dma(K - 3, NQ), dma(K - 3, NQ),
            dma(5, ND), dma(5, ND), dma(10),
        ],
        compiler_params=pltpu.CompilerParams(
            collective_id=0, has_side_effects=True, vmem_limit_bytes=26 * 1024 * 1024
        ),
    )(*[pltpu.with_memory_space_constraint(v, pltpu.HBM) for v in (tokens, block_weight, left_factor, right_factor, out_cotangent)])
    results = (act, ig, wg, lg, rg)
    act, ig, wg, lg, rg = pl.pallas_call(
        hand_over,
        out_shape=tuple(out(*x.shape) for x in results),
        in_specs=[pl.BlockSpec(memory_space=pltpu.VMEM)] * 5,
        out_specs=[pl.BlockSpec(memory_space=pltpu.HBM)] * 5,
        scratch_shapes=[dma(5)],
        compiler_params=pltpu.CompilerParams(vmem_limit_bytes=4 * 1024 * 1024),
    )(*results)
    return act, ig, wg, lg.reshape(C, R), rg.reshape(R, H)


def solution(mesh):
    return jax.shard_map(
        on_device,
        mesh=mesh,
        in_specs=(P("dp", "mp"), P(None, None, "mp"), P("mp", None), P(None, "mp"), P("dp", "mp")),
        out_specs=(P("dp", "mp"), P("dp", "mp"), P(None, "dp", "mp"), P("mp", None), P(None, "mp")),
        check_vma=False,
    )
```
